256 devices in a mesh: pipe: 8 (over z_lo, core), seq: 32 (over z_hi, y, x).
Axes of the slice: x: 4, y: 4, z: 8 (z_hi: 2, z_lo: 4; z = z_hi * 4 + z_lo), core: 2. Of those that a mesh axis runs over, the one named last changes fastest.
Arguments:
- queries: bfloat16 [8, 4096, 12288], P('pipe', 'seq'), may hold values from -6 to 6
- keys: bfloat16 [8, 4096, 12288], P('pipe', 'seq'), may hold values from -6 to 6
- values: bfloat16 [8, 4096, 8192], P('pipe', 'seq'), may hold values from -6 to 6
- doc_lengths: int32 [8, 16], replicated, may hold values from 1 to 512, 4096 in all within a row
Outputs:
- mtp_attention: bfloat16 [8, 4096, 8192], P('pipe', 'seq')
The draws below stay inside these ranges and needn't reach their ends.
All inputs are finite; a program needn't handle non-finite values.
Results may differ from the reference program's by a relative error of at most 0.0046.
Values may be sent and summed in bfloat16 or wider, within the bound.
No kernel may reach another device: no remote copies, remote signals or barrier semaphores. Data moves between devices by JAX's collectives and lax.ppermute only.
A program may use at most 128 MiB of HBM per device.

```python
import math
from functools import partial
import jax
import jax.numpy as jnp
import numpy as np
from jax import lax

HEADS = 64
DQK = 192
DV = 128
DOCS = 16
LENGTH = 4096
MICRO = 8
MOST = 512


def shared_fields(key):
    shape = (MICRO, LENGTH, HEADS, DQK)
    query_key = jax.random.fold_in(key, 11)
    key_key = jax.random.fold_in(key, 12)
    query_field = jnp.clip(jax.random.normal(query_key, shape, jnp.float32), -4.0, 4.0)
    key_field = jnp.clip(jax.random.normal(key_key, shape, jnp.float32), -4.0, 4.0)
    return (query_field.reshape(MICRO, LENGTH, HEADS * DQK), key_field.reshape(MICRO, LENGTH, HEADS * DQK))


def draw_queries(key, part):
    return shared_fields(key)[0].astype(jnp.bfloat16)


def draw_keys(key, part):
    return shared_fields(key)[1].astype(jnp.bfloat16)


def block_levels(rng, extent, split, low, top_value):
    loudness, own = 1.0, jax.random.fold_in(rng, 6)
    for axis_at, blocks in split:
        draws = jnp.exp(jax.random.uniform(jax.random.fold_in(own, axis_at), (blocks,), jnp.float32, low / len(split), top_value / len(split)))
        loudness = loudness * jnp.repeat(draws, extent[axis_at] // blocks).reshape([-1 if axis == axis_at else 1 for axis in range(len(extent))])
    return loudness


def profile(amount, total, bound, slope):
    portions = [(1 << 20) // math.isqrt(standing ** slope) + 1 for standing in range(2, amount + 1)]
    surplus, given = total - bound - (amount - 1), [1] * (amount - 1)
    while surplus > 0:
        movable = [i for i in range(amount - 1) if given[i] < bound]
        whole, remaining = sum([portions[i] for i in movable]), surplus
        for i in movable:
            more = min(bound - given[i], max(1, remaining * portions[i] // whole), surplus)
            given[i] = given[i] + more
            surplus = surplus - more
    return np.array([bound] + given)


def uneven_parts(rng, count, total, limit, slope):
    if count == 2:
        one = jax.random.randint(rng, (), max(1, total - limit), min(limit, total - 1) + 1)
        return jnp.stack([one, total - one])
    tallies = jnp.asarray(profile(count, total, limit, slope), jnp.int32)
    twos = (count - 1) // 2
    donor, receiver = tallies[1:1 + 2 * twos:2], tallies[2:2 + 2 * twos:2]
    room = jnp.minimum(donor - 1, limit - receiver)
    moved = jax.random.randint(jax.random.fold_in(rng, 1), (twos,), 0, 1 << 20) % (room + 1)
    tallies = tallies.at[1:1 + 2 * twos:2].set(donor - moved).at[2:2 + 2 * twos:2].set(receiver + moved)
    return tallies[jax.random.permutation(jax.random.fold_in(rng, 2), count)]


def scatter_about(own_key, extent, scale, reach, cuts=(), held_as=jnp.bfloat16):
    values = scale * jax.random.normal(own_key, extent, jnp.float32)
    if cuts:
        values = values * block_levels(own_key, extent, cuts, -0.22, 0.18)
    return jnp.clip(values, -reach, reach).astype(held_as)


def setup_inputs(seed: int = 0) -> dict:
    streams_of = jax.random.split(jax.random.key(seed), 5)
    return {
        "queries": draw_queries(jax.random.fold_in(streams_of[4], 71), 0),
        "keys": draw_keys(jax.random.fold_in(streams_of[4], 71), 0),
        "values": scatter_about(streams_of[2], (MICRO, LENGTH, HEADS * DV), 1.0, 6.0, ((0, 8), (1, 32))),
        "doc_lengths": jax.vmap(lambda own: uneven_parts(own, DOCS, LENGTH, MOST, 2))(jax.random.split(streams_of[3], MICRO)).reshape((MICRO, DOCS)).astype(jnp.int32),
    }


def attend_head(parts, visible):
    query_head, key_head, value_head = parts
    scores = jnp.dot(query_head, key_head.T, preferred_element_type=jnp.float32) * (DQK ** -0.5)
    scores = jnp.where(visible, scores, -jnp.inf)
    row_max = jnp.max(scores, axis=1, keepdims=True)
    exponent = jnp.exp(scores - row_max)
    weights = (exponent / jnp.sum(exponent, axis=1, keepdims=True)).astype(jnp.bfloat16)
    return jnp.dot(weights, value_head, preferred_element_type=jnp.float32).astype(jnp.bfloat16)


def reference(queries, keys, values, doc_lengths):
    position = jnp.arange(LENGTH, dtype=jnp.int32)
    results = []
    for number in range(MICRO):
        doc_ends = jnp.cumsum(doc_lengths[number]).astype(jnp.int32)
        document = jnp.sum((doc_ends[None, :] <= position[:, None]).astype(jnp.int32), axis=1)
        visible = (document[:, None] == document[None, :]) & (position[None, :] <= position[:, None])
        query_heads = queries[number].reshape(LENGTH, HEADS, DQK).transpose(1, 0, 2)
        key_heads = keys[number].reshape(LENGTH, HEADS, DQK).transpose(1, 0, 2)
        value_heads = values[number].reshape(LENGTH, HEADS, DV).transpose(1, 0, 2)
        attended = lax.map(partial(attend_head, visible=visible), (query_heads, key_heads, value_heads))
        results.append(attended.transpose(1, 0, 2).reshape(LENGTH, HEADS * DV))
    stacked = jnp.stack(results)
    return jnp.roll(stacked, 1, axis=0)
```

```python
import functools
import jax
import jax.numpy as jnp
from jax import lax
from jax.experimental import pallas as pl
from jax.experimental.pallas import tpu as pltpu
from jax.sharding import PartitionSpec as P

HEADS = 64
DQK = 192
DV = 128
DOCS = 16
LONGEST = 512
BLOCK = 128
CHUNKS = 2
GROUP = 16
NEGATIVE = -1e30


def attention_kernel(doc_starts, base, query, key_value, edge, out, window, sems):
    rows = query.shape[0]
    copies = (
        pltpu.make_async_copy(edge, window.at[pl.ds(0, LONGEST)], sems.at[0]),
        pltpu.make_async_copy(key_value, window.at[pl.ds(LONGEST, rows)], sems.at[1]),
    )
    for copy in copies:
        copy.start()
    for copy in copies:
        copy.wait()
    span = LONGEST + BLOCK
    first = base[0]
    lane = lax.broadcasted_iota(jnp.int32, (BLOCK, BLOCK), 1)
    sublane = lax.broadcasted_iota(jnp.int32, (BLOCK, BLOCK), 0)
    column = lax.broadcasted_iota(jnp.int32, (BLOCK, 256), 1)
    scale = DQK ** (-0.5)

    def block(number, carry):
        row = pl.multiple_of(number * BLOCK, BLOCK)
        position = first + row + sublane
        start = jnp.zeros((BLOCK, BLOCK), jnp.int32)
        for doc in range(1, DOCS):
            begin = doc_starts[doc]
            start = jnp.where(position >= begin, begin, start)
        start = start - (first + row - LONGEST)
        for head in range(2):
            queries = query[pl.ds(row, BLOCK), 128 * head : 128 * head + 256]
            inside = column < DQK if head == 0 else column >= 256 - DQK
            queries = jnp.where(inside, queries, jnp.zeros_like(queries))
            keys = window[pl.ds(row, span), 128 * head : 128 * head + 256]
            values = window[pl.ds(row, span), 384 + 128 * head : 512 + 128 * head]
            scores = lax.dot_general(
                queries, keys, (((1,), (1,)), ((), ())), preferred_element_type=jnp.float32
            )
            parts = []
            for part in range(span // BLOCK):
                piece = scores[:, part * BLOCK : (part + 1) * BLOCK]
                visible = lane + part * BLOCK >= start
                if part == span // BLOCK - 1:
                    visible = visible & (lane <= sublane)
                parts.append(jnp.where(visible, piece, NEGATIVE))
            scores = jnp.concatenate(parts, axis=1)
            top = jnp.max(scores, axis=1, keepdims=True)
            exponent = jnp.exp((scores - top) * scale)
            total = jnp.sum(exponent, axis=1, keepdims=True)
            weights = (exponent * (1.0 / total)).astype(jnp.bfloat16)
            mixed = jnp.dot(weights, values, preferred_element_type=jnp.float32)
            out[pl.ds(row, BLOCK), DV * head : DV * (head + 1)] = mixed.astype(jnp.bfloat16)
        return carry

    lax.fori_loop(0, rows // BLOCK, block, 0)


def attention(doc_starts, base, query, key_value, edge):
    rows = query.shape[0]
    return pl.pallas_call(
        attention_kernel,
        out_shape=jax.ShapeDtypeStruct((rows, 2 * DV), jnp.bfloat16),
        in_specs=[
            pl.BlockSpec(memory_space=pltpu.SMEM),
            pl.BlockSpec(memory_space=pltpu.SMEM),
            pl.BlockSpec(memory_space=pltpu.VMEM),
            pl.BlockSpec(memory_space=pl.ANY),
            pl.BlockSpec(memory_space=pl.ANY),
        ],
        out_specs=pl.BlockSpec(memory_space=pltpu.VMEM),
        scratch_shapes=[
            pltpu.VMEM((LONGEST + rows, 640), jnp.bfloat16),
            pltpu.SemaphoreType.DMA((2,)),
        ],
        name="attention",
    )(doc_starts, base, query, key_value, edge)


def exchange(block):
    groups = [[half * GROUP + i for i in range(GROUP)] for half in range(2)]
    return lax.all_to_all(
        block, "seq", split_axis=0, concat_axis=0, axis_index_groups=groups, tiled=True
    )


def local(queries, keys, values, doc_lengths):
    segment = lax.axis_index("pipe")
    half = lax.axis_index("seq") // GROUP
    lengths = lax.dynamic_index_in_dim(doc_lengths, segment, 0, keepdims=False)
    doc_starts = jnp.cumsum(lengths) - lengths
    rows = queries.shape[1]
    base = (half * GROUP * rows).astype(jnp.int32).reshape(1)
    heads = HEADS // CHUNKS // GROUP

    def chunk(array, number, width):
        columns = HEADS // CHUNKS * width
        piece = array[0, :, number * columns : (number + 1) * columns]
        return piece.reshape(rows, GROUP, heads * width).transpose(1, 0, 2)

    results = []
    for number in range(CHUNKS):
        key_value = jnp.concatenate(
            [chunk(keys, number, DQK), chunk(values, number, DV)], axis=2
        )
        key_value = exchange(key_value).reshape(GROUP * rows, heads * (DQK + DV))
        query = exchange(chunk(queries, number, DQK)).reshape(GROUP * rows, heads * DQK)
        edge = lax.ppermute(
            key_value[-LONGEST:], "seq", [(i, i + GROUP) for i in range(GROUP)]
        )
        attended = attention(doc_starts, base, query, key_value, edge)
        attended = exchange(attended.reshape(GROUP, rows, heads * DV))
        shifted = lax.ppermute(attended, "pipe", [(i, (i + 1) % 8) for i in range(8)])
        results.append(shifted.transpose(1, 0, 2).reshape(1, rows, HEADS // CHUNKS * DV))
    return jnp.concatenate(results, axis=2)


def solution(mesh):
    placed = (P("pipe", "seq", None), P("pipe", "seq", None), P("pipe", "seq", None), P())
    return jax.shard_map(
        local, mesh=mesh, in_specs=placed, out_specs=P("pipe", "seq", None), check_vma=False
    )
```

```python
import functools
import jax
import jax.numpy as jnp
from jax import lax
from jax.experimental import pallas as pl
from jax.experimental.pallas import tpu as pltpu
from jax.sharding import PartitionSpec as P

HEADS = 64
DQK = 192
DV = 128
DOCS = 16
LONGEST = 512
BLOCK = 256
LANES = 128
CHUNKS = 2
SIDE = 4
GROUP = SIDE * SIDE
PER = HEADS // CHUNKS // GROUP
WQK = PER * DQK
WV = PER * DV
WKV = WQK + WV
NEGATIVE = -1e30
ANY = pl.BlockSpec(memory_space=pl.ANY)
SMEM = pl.BlockSpec(memory_space=pltpu.SMEM)


def run_copies(copies):
    for copy in copies:
        copy.start()
    for copy in copies:
        copy.wait()


def member_of(place, order, first, second, sign):
    ahead, aside = (second, first) if order == "xy" else (first, second)
    y = lax.rem(place[0] + SIDE + sign * ahead, SIDE)
    x = lax.rem(place[1] + SIDE + sign * aside, SIDE)
    return y * SIDE + x


def pack_kernel(plan, order, place, *refs):
    count = len(plan)
    sources, targets = refs[:count], refs[count : count + SIDE]
    buffer, in_sems, out_sems = refs[count + SIDE :]
    arriving, leaving = [], []
    for first in range(SIDE):
        group = []
        for second in range(SIDE):
            member = member_of(place, order, first, second, 1)
            for number, (source, (begin, width, at)) in enumerate(zip(sources, plan)):
                column = pl.multiple_of(begin + member * width, 128)
                group.append(
                    pltpu.make_async_copy(
                        source.at[0, :, pl.ds(column, width)],
                        buffer.at[first, second, :, pl.ds(at, width)],
                        in_sems.at[first, second, number],
                    )
                )
        arriving.append(group)
        leaving.append(pltpu.make_async_copy(buffer.at[first], targets[first], out_sems.at[first]))
    for group in arriving:
        for copy in group:
            copy.start()
    for first in range(SIDE):
        for copy in arriving[first]:
            copy.wait()
        leaving[first].start()
    for copy in leaving:
        copy.wait()


def pack(place, order, parts):
    rows = parts[0][0].shape[1]
    plan, at = [], 0
    for _, first, width in parts:
        plan.append((first, width, at))
        at += width
    return pl.pallas_call(
        functools.partial(pack_kernel, tuple(plan), order),
        out_shape=[jax.ShapeDtypeStruct((SIDE, rows, at), jnp.bfloat16)] * SIDE,
        in_specs=[SMEM] + [ANY] * len(parts),
        out_specs=[ANY] * SIDE,
        scratch_shapes=[
            pltpu.VMEM((SIDE, SIDE, rows, at), jnp.bfloat16),
            pltpu.SemaphoreType.DMA((SIDE, SIDE, len(parts))),
            pltpu.SemaphoreType.DMA((SIDE,)),
        ],
        name="pack",
    )(place, *[part[0] for part in parts])


def repack_kernel(begin, *refs):
    sources, targets = refs[:SIDE], refs[SIDE:-3]
    buffer, in_sems, out_sems = refs[-3:]
    count = SIDE - begin
    run_copies(
        [
            pltpu.make_async_copy(
                sources[first].at[pl.ds(begin, count)], buffer.at[:, first], in_sems.at[first]
            )
            for first in range(SIDE)
        ]
    )
    run_copies(
        [
            pltpu.make_async_copy(buffer.at[second], targets[second], out_sems.at[second])
            for second in range(count)
        ]
    )


def repack(arrays, begin):
    shape = arrays[0].shape
    count = SIDE - begin
    return pl.pallas_call(
        functools.partial(repack_kernel, begin),
        out_shape=[jax.ShapeDtypeStruct(shape, jnp.bfloat16)] * count,
        in_specs=[ANY] * SIDE,
        out_specs=[ANY] * count,
        scratch_shapes=[
            pltpu.VMEM((count,) + shape, jnp.bfloat16),
            pltpu.SemaphoreType.DMA((SIDE,)),
            pltpu.SemaphoreType.DMA((count,)),
        ],
        name="repack",
    )(*arrays)


def send(block, axis, distance, shifted=False):
    routes = []
    for half in range(2):
        for y in range(SIDE):
            for x in range(SIDE):
                to_y = (y + distance) % SIDE if axis == "y" else y
                to_x = (x + distance) % SIDE if axis == "x" else x
                routes.append((half * GROUP + y * SIDE + x, half * GROUP + to_y * SIDE + to_x))
    if not shifted:
        return lax.ppermute(block, "seq", routes)
    segments, members = lax.axis_size("pipe"), lax.axis_size("seq")
    routes = [
        (segment * members + a, (segment + 1) % segments * members + b)
        for segment in range(segments)
        for a, b in routes
    ]
    return lax.ppermute(block, ("pipe", "seq"), routes)


def first_stage(arrays, order):
    return [arrays[0]] + [send(arrays[i], order[0], i) for i in range(1, SIDE)]


def second_stage(arrays, order, shifted=False):
    if shifted:
        got = [send(array, order[1], i, True) for i, array in enumerate(repack(arrays, 0))]
    else:
        got = [send(array, order[1], i + 1) for i, array in enumerate(repack(arrays, 1))]
        got = list(arrays) + got
    table = {}
    for first in range(SIDE):
        for second in range(SIDE):
            key = (second, first) if order == "xy" else (first, second)
            if shifted:
                table[key] = (second, first)
            elif second == 0:
                table[key] = (first, 0)
            else:
                table[key] = (SIDE + second - 1, first)
    return got, table


def edge_kernel(table, place, *refs):
    sources, (target, buffer, sems) = refs[:-3], refs[-3:]
    last = lax.rem(place[0] + 1, SIDE)
    for ahead in range(SIDE):

        @pl.when(last == ahead)
        def _():
            copies = []
            for aside in range(SIDE):
                array, at = table[(ahead, aside)]
                copies.append(
                    pltpu.make_async_copy(sources[array].at[at], buffer.at[aside], sems.at[aside])
                )
            run_copies(copies)

    run_copies([pltpu.make_async_copy(buffer, target, sems.at[0])])


def send_edge(place, arrays, table):
    shape = arrays[0].shape
    edge = pl.pallas_call(
        functools.partial(edge_kernel, table),
        out_shape=jax.ShapeDtypeStruct(shape, jnp.bfloat16),
        in_specs=[SMEM] + [ANY] * len(arrays),
        out_specs=ANY,
        scratch_shapes=[pltpu.VMEM(shape, jnp.bfloat16), pltpu.SemaphoreType.DMA((SIDE,))],
        name="edge",
    )(place, *arrays)
    return lax.ppermute(edge, "seq", [(i, i + GROUP) for i in range(GROUP)])


def place_kernel(first, table, place, *refs):
    count = max(array for array, _ in table.values()) + 1
    pieces = refs[:count]
    target, buffer, in_sems, out_sem = refs[-4:]
    width = pieces[0].shape[2]
    copies = []
    for (ahead, aside), (array, at) in table.items():
        member = member_of(place, "yx", ahead, aside, -1)
        column = pl.multiple_of(member * width, 128)
        copies.append(
            pltpu.make_async_copy(
                pieces[array].at[at], buffer.at[:, pl.ds(column, width)], in_sems.at[array, at]
            )
        )
    run_copies(copies)
    run_copies(
        [pltpu.make_async_copy(buffer, target.at[0, :, pl.ds(first, GROUP * width)], out_sem.at[0])]
    )


def put(place, arrays, table, first, columns, whole=None):
    _, rows, width = arrays[0].shape
    extra = [] if whole is None else [whole]
    return pl.pallas_call(
        functools.partial(place_kernel, first, table),
        out_shape=jax.ShapeDtypeStruct((1, rows, columns), jnp.bfloat16),
        in_specs=[SMEM] + [ANY] * (len(arrays) + len(extra)),
        out_specs=ANY,
        scratch_shapes=[
            pltpu.VMEM((rows, GROUP * width), jnp.bfloat16),
            pltpu.SemaphoreType.DMA((len(arrays), SIDE)),
            pltpu.SemaphoreType.DMA((1,)),
        ],
        input_output_aliases={len(arrays) + 1: 0} if extra else {},
        name="place",
    )(place, *arrays, *extra)


def latest_start(doc_starts, position):
    start = jnp.zeros_like(position)
    for doc in range(1, DOCS):
        start = jnp.where(position >= doc_starts[doc], doc_starts[doc], start)
    return start


def attend(doc_starts, first_position, queries_in, window, mixed_out):
    lane = lax.broadcasted_iota(jnp.int32, (BLOCK, LANES), 1)
    sublane = lax.broadcasted_iota(jnp.int32, (BLOCK, LANES), 0)
    column = lax.broadcasted_iota(jnp.int32, (BLOCK, 2 * LANES), 1)
    scale = DQK ** (-0.5)

    def heads(row, start, span):
        above = LONGEST + BLOCK - span
        begin = pl.multiple_of(row + above, LANES)
        start = start - (first_position + row - LONGEST + above)
        masks = []
        for part in range(span // LANES):
            visible = lane + part * LANES >= start
            if part * LANES >= span - BLOCK:
                visible = visible & (lane + (part * LANES - (span - BLOCK)) <= sublane)
            masks.append(visible)
        mask = jnp.concatenate(masks, axis=1)
        scores, values = [], []
        for head in range(PER):
            columns = slice(LANES * head, LANES * head + 2 * LANES)
            query = queries_in[pl.ds(row, BLOCK), columns]
            inside = column < DQK if head == 0 else column >= 2 * LANES - DQK
            query = jnp.where(inside, query, jnp.zeros_like(query))
            scores.append(
                lax.dot_general(
                    query,
                    window[pl.ds(begin, span), columns],
                    (((1,), (1,)), ((), ())),
                    preferred_element_type=jnp.float32,
                )
            )
            values.append(window[pl.ds(begin, span), WQK + DV * head : WQK + DV * (head + 1)])
        scores = [jnp.where(mask, score, NEGATIVE) for score in scores]
        tops = [jnp.max(score, axis=1, keepdims=True) for score in scores]
        exponents = [jnp.exp((score - top) * scale) for score, top in zip(scores, tops)]
        totals = [jnp.sum(exponent, axis=1, keepdims=True) for exponent in exponents]
        weights = [
            (exponent * (1.0 / total)).astype(jnp.bfloat16)
            for exponent, total in zip(exponents, totals)
        ]
        for head in range(PER):
            mixed = jnp.dot(weights[head], values[head], preferred_element_type=jnp.float32)
            mixed_out[pl.ds(row, BLOCK), DV * head : DV * (head + 1)] = mixed.astype(jnp.bfloat16)

    def block(number, carry):
        row = pl.multiple_of(number * BLOCK, BLOCK)
        position = first_position + row
        start = latest_start(doc_starts, position + sublane)
        back = position - latest_start(doc_starts, position)
        extra = (back + LANES - 1) // LANES
        for count in range(LONGEST // LANES + 1):
            pl.when(extra == count)(
                functools.partial(heads, row, start, BLOCK + count * LANES)
            )
        return carry

    lax.fori_loop(0, queries_in.shape[0] // BLOCK, block, 0)


def attention_kernel(plan, doc_starts, place, *refs):
    query_table, key_table, order, query_count, key_count = plan
    queries, keys = refs[:query_count], refs[query_count : query_count + key_count]
    edge = refs[query_count + key_count]
    targets = refs[query_count + key_count + 1 :][:SIDE]
    queries_in, window, mixed_out, sems, edge_sems = refs[-5:]
    rows = queries_in.shape[0]
    block_rows = rows // GROUP
    copies = []
    for (ahead, aside), (array, at) in query_table.items():
        row = pl.multiple_of(member_of(place, "yx", ahead, aside, -1) * block_rows, block_rows)
        copies.append(
            pltpu.make_async_copy(
                queries[array].at[at], queries_in.at[pl.ds(row, block_rows)], sems.at[0, ahead, aside]
            )
        )
        array, at = key_table[(ahead, aside)]
        copies.append(
            pltpu.make_async_copy(
                keys[array].at[at],
                window.at[pl.ds(LONGEST + row, block_rows)],
                sems.at[1, ahead, aside],
            )
        )
    for aside in range(SIDE):
        row = pl.multiple_of(lax.rem(place[1] + SIDE - aside, SIDE) * block_rows, block_rows)
        copies.append(
            pltpu.make_async_copy(
                edge.at[aside], window.at[pl.ds(row, block_rows)], edge_sems.at[aside]
            )
        )
    run_copies(copies)
    attend(doc_starts, place[2], queries_in, window, mixed_out)
    copies = []
    for first in range(SIDE):
        for second in range(SIDE):
            row = pl.multiple_of(member_of(place, order, first, second, 1) * block_rows, block_rows)
            copies.append(
                pltpu.make_async_copy(
                    mixed_out.at[pl.ds(row, block_rows)],
                    targets[first].at[second],
                    sems.at[0, first, second],
                )
            )
    run_copies(copies)


def attention(doc_starts, place, query, key_value, edge, order):
    (queries, query_table), (keys, key_table) = query, key_value
    block_rows = keys[0].shape[1]
    rows = GROUP * block_rows
    plan = (query_table, key_table, order, len(queries), len(keys))
    return pl.pallas_call(
        functools.partial(attention_kernel, plan),
        out_shape=[jax.ShapeDtypeStruct((SIDE, block_rows, WV), jnp.bfloat16)] * SIDE,
        in_specs=[SMEM, SMEM] + [ANY] * (len(queries) + len(keys) + 1),
        out_specs=[ANY] * SIDE,
        scratch_shapes=[
            pltpu.VMEM((rows, WQK), jnp.bfloat16),
            pltpu.VMEM((LONGEST + rows, WKV), jnp.bfloat16),
            pltpu.VMEM((rows, WV), jnp.bfloat16),
            pltpu.SemaphoreType.DMA((2, SIDE, SIDE)),
            pltpu.SemaphoreType.DMA((SIDE,)),
        ],
        name="attention",
    )(doc_starts, place, *queries, *keys, edge)


def together(*arrays):
    return lax.optimization_barrier(arrays)


def local(queries, keys, values, doc_lengths):
    segment = lax.axis_index("pipe")
    seq = lax.axis_index("seq")
    doc_starts = jnp.cumsum(doc_lengths, axis=1) - doc_lengths
    doc_starts = lax.dynamic_index_in_dim(doc_starts, segment, 0, keepdims=False)
    rows = queries.shape[1]
    half, member = seq // GROUP, seq % GROUP
    place = jnp.stack([member // SIDE, member % SIDE, half * (GROUP * rows)]).astype(jnp.int32)
    columns = HEADS * DV
    second_qk, second_v = HEADS * DQK // 2, HEADS * DV // 2

    kv = [
        first_stage(pack(place, "xy", [(keys, 0, WQK), (values, 0, WV)]), "xy"),
        first_stage(pack(place, "yx", [(keys, second_qk, WQK), (values, second_v, WV)]), "yx"),
    ]
    q = [
        first_stage(pack(place, "xy", [(queries, 0, WQK)]), "xy"),
        first_stage(pack(place, "yx", [(queries, second_qk, WQK)]), "yx"),
    ]
    kv = [second_stage(kv[0], "xy"), second_stage(kv[1], "yx")]
    edges = [send_edge(place, *kv[0]), send_edge(place, *kv[1])]
    q = [second_stage(q[0], "xy"), second_stage(q[1], "yx")]
    whole = None
    for number, order in enumerate(("xy", "yx")):
        out = attention(doc_starts, place, q[number], kv[number], edges[number], order)
        out, table = second_stage(first_stage(out, order), order, True)
        whole = put(place, out, table, number * second_v, columns, whole)
    return whole


def solution(mesh):
    placed = (P("pipe", "seq", None), P("pipe", "seq", None), P("pipe", "seq", None), P())
    return jax.shard_map(
        local, mesh=mesh, in_specs=placed, out_specs=P("pipe", "seq", None), check_vma=False
    )
```

```python
import functools
import jax
import jax.numpy as jnp
from jax import lax
from jax.experimental import pallas as pl
from jax.experimental.pallas import tpu as pltpu
from jax.sharding import PartitionSpec as P

HEADS = 64
DQK = 192
DV = 128
DOCS = 16
LONGEST = 512
BLOCK = 256
LANES = 128
EXTRA = (128, 256, 512)
CHUNKS = 2
SIDE = 4
GROUP = SIDE * SIDE
PER = HEADS // CHUNKS // GROUP
WQK = PER * DQK
WV = PER * DV
WKV = WQK + WV
NEGATIVE = -1e30
ANY = pl.BlockSpec(memory_space=pl.ANY)
SMEM = pl.BlockSpec(memory_space=pltpu.SMEM)


def run_copies(copies):
    for copy in copies:
        copy.start()
    for copy in copies:
        copy.wait()


def run_some(copies):
    for wanted, copy in copies:
        pl.when(wanted)(copy.start)
    for wanted, copy in copies:
        pl.when(wanted)(copy.wait)


def member_of(place, order, first, second, sign):
    ahead, aside = (second, first) if order == "xy" else (first, second)
    y = lax.rem(place[0] + SIDE + sign * ahead, SIDE)
    x = lax.rem(place[1] + SIDE + sign * aside, SIDE)
    return y * SIDE + x


def pack_kernel(plan, order, place, *refs):
    count = len(plan)
    sources, targets = refs[:count], refs[count : count + SIDE]
    buffer, in_sems, out_sems = refs[count + SIDE :]
    arriving, leaving = [], []
    for first in range(SIDE):
        group = []
        for second in range(SIDE):
            member = member_of(place, order, first, second, 1)
            for number, (source, (begin, width, at)) in enumerate(zip(sources, plan)):
                column = pl.multiple_of(begin + member * width, 128)
                group.append(
                    pltpu.make_async_copy(
                        source.at[0, :, pl.ds(column, width)],
                        buffer.at[first, second, :, pl.ds(at, width)],
                        in_sems.at[first, second, number],
                    )
                )
        arriving.append(group)
        leaving.append(pltpu.make_async_copy(buffer.at[first], targets[first], out_sems.at[first]))
    for group in arriving:
        for copy in group:
            copy.start()
    for first in range(SIDE):
        for copy in arriving[first]:
            copy.wait()
        leaving[first].start()
    for copy in leaving:
        copy.wait()


def pack(place, order, parts):
    rows = parts[0][0].shape[1]
    plan, at = [], 0
    for _, first, width in parts:
        plan.append((first, width, at))
        at += width
    return pl.pallas_call(
        functools.partial(pack_kernel, tuple(plan), order),
        out_shape=[jax.ShapeDtypeStruct((SIDE, rows, at), jnp.bfloat16)] * SIDE,
        in_specs=[SMEM] + [ANY] * len(parts),
        out_specs=[ANY] * SIDE,
        scratch_shapes=[
            pltpu.VMEM((SIDE, SIDE, rows, at), jnp.bfloat16),
            pltpu.SemaphoreType.DMA((SIDE, SIDE, len(parts))),
            pltpu.SemaphoreType.DMA((SIDE,)),
        ],
        name="pack",
    )(place, *[part[0] for part in parts])


def repack_kernel(begin, *refs):
    sources, targets = refs[:SIDE], refs[SIDE:-3]
    buffer, in_sems, out_sems = refs[-3:]
    count = SIDE - begin
    run_copies(
        [
            pltpu.make_async_copy(
                sources[first].at[pl.ds(begin, count)], buffer.at[:, first], in_sems.at[first]
            )
            for first in range(SIDE)
        ]
    )
    run_copies(
        [
            pltpu.make_async_copy(buffer.at[second], targets[second], out_sems.at[second])
            for second in range(count)
        ]
    )


def repack(arrays, begin):
    shape = arrays[0].shape
    count = SIDE - begin
    return pl.pallas_call(
        functools.partial(repack_kernel, begin),
        out_shape=[jax.ShapeDtypeStruct(shape, jnp.bfloat16)] * count,
        in_specs=[ANY] * SIDE,
        out_specs=[ANY] * count,
        scratch_shapes=[
            pltpu.VMEM((count,) + shape, jnp.bfloat16),
            pltpu.SemaphoreType.DMA((SIDE,)),
            pltpu.SemaphoreType.DMA((count,)),
        ],
        name="repack",
    )(*arrays)


def send(block, axis, distance, shifted=False):
    return routed(block, axis, distance, shifted)


def routed(block, axis, distance, shifted):
    routes = []
    for half in range(2):
        for y in range(SIDE):
            for x in range(SIDE):
                to_y = (y + distance) % SIDE if axis == "y" else y
                to_x = (x + distance) % SIDE if axis == "x" else x
                routes.append((half * GROUP + y * SIDE + x, half * GROUP + to_y * SIDE + to_x))
    if not shifted:
        return lax.ppermute(block, "seq", routes)
    segments, members = lax.axis_size("pipe"), lax.axis_size("seq")
    routes = [
        (segment * members + a, (segment + 1) % segments * members + b)
        for segment in range(segments)
        for a, b in routes
    ]
    return lax.ppermute(block, ("pipe", "seq"), routes)


def shift(block):
    segments = lax.axis_size("pipe")
    return lax.ppermute(block, "pipe", [(i, (i + 1) % segments) for i in range(segments)])


def first_stage(arrays, order, shifted=False):
    if shifted:
        return [send(array, order[0], i, True) for i, array in enumerate(arrays)]
    return [arrays[0]] + [send(arrays[i], order[0], i) for i in range(1, SIDE)]


def second_stage(arrays, order):
    got = [send(array, order[1], i + 1) for i, array in enumerate(repack(arrays, 1))]
    got = list(arrays) + got
    table = {}
    for first in range(SIDE):
        for second in range(SIDE):
            key = (second, first) if order == "xy" else (first, second)
            if second == 0:
                table[key] = (first, 0)
            else:
                table[key] = (SIDE + second - 1, first)
    return got, table


def edge_kernel(table, place, *refs):
    sources, (target, buffer, sems) = refs[:-3], refs[-3:]
    last = lax.rem(place[0] + 1, SIDE)
    for ahead in range(SIDE):

        @pl.when(last == ahead)
        def _():
            copies = []
            for aside in range(SIDE):
                array, at = table[(ahead, aside)]
                copies.append(
                    pltpu.make_async_copy(sources[array].at[at], buffer.at[aside], sems.at[aside])
                )
            run_copies(copies)

    run_copies([pltpu.make_async_copy(buffer, target, sems.at[0])])


def send_edge(place, arrays, table):
    shape = arrays[0].shape
    edge = pl.pallas_call(
        functools.partial(edge_kernel, table),
        out_shape=jax.ShapeDtypeStruct(shape, jnp.bfloat16),
        in_specs=[SMEM] + [ANY] * len(arrays),
        out_specs=ANY,
        scratch_shapes=[pltpu.VMEM(shape, jnp.bfloat16), pltpu.SemaphoreType.DMA((SIDE,))],
        name="edge",
    )(place, *arrays)
    return lax.ppermute(edge, "seq", [(i, i + GROUP) for i in range(GROUP)])


def place_kernel(first, table, place, *refs):
    target, buffer, in_sems, out_sem = refs[-4:]
    width = refs[0].shape[2]
    pieces = refs
    copies = []
    if table is None:
        table = {(0, at): (0, at) for at in range(GROUP)}
    for (ahead, aside), (array, at) in table.items():
        member = aside
        if pieces[0].shape[0] != GROUP:
            member = member_of(place, "yx", ahead, aside, -1)
        column = pl.multiple_of(member * width, 128)
        copies.append(
            pltpu.make_async_copy(
                pieces[array].at[at], buffer.at[:, pl.ds(column, width)], in_sems.at[array, at]
            )
        )
    run_copies(copies)
    run_copies(
        [pltpu.make_async_copy(buffer, target.at[0, :, pl.ds(first, GROUP * width)], out_sem.at[0])]
    )


def put(place, arrays, table, first, columns, whole=None):
    _, rows, width = arrays[0].shape
    extra = [] if whole is None else [whole]
    return pl.pallas_call(
        functools.partial(place_kernel, first, table),
        out_shape=jax.ShapeDtypeStruct((1, rows, columns), jnp.bfloat16),
        in_specs=[SMEM] + [ANY] * (len(arrays) + len(extra)),
        out_specs=ANY,
        scratch_shapes=[
            pltpu.VMEM((rows, GROUP * width), jnp.bfloat16),
            pltpu.SemaphoreType.DMA((len(arrays), GROUP)),
            pltpu.SemaphoreType.DMA((1,)),
        ],
        input_output_aliases={len(arrays) + 1: 0} if extra else {},
        name="place",
    )(place, *arrays, *extra)


def latest_start(doc_starts, position):
    start = jnp.zeros_like(position)
    for doc in range(1, DOCS):
        start = jnp.where(position >= doc_starts[doc], doc_starts[doc], start)
    return start


def attend(doc_starts, first_position, queries_in, window, mixed_out, first, last):
    lane = lax.broadcasted_iota(jnp.int32, (BLOCK, LANES), 1)
    sublane = lax.broadcasted_iota(jnp.int32, (BLOCK, LANES), 0)
    column = lax.broadcasted_iota(jnp.int32, (BLOCK, 2 * LANES), 1)
    scale = DQK ** (-0.5)

    def heads(row, start, span):
        above = LONGEST + BLOCK - span
        begin = pl.multiple_of(row + above, LANES)
        start = start - (first_position + row - LONGEST + above)
        masks = []
        for part in range(span // LANES):
            visible = lane + part * LANES >= start
            if part * LANES >= span - BLOCK:
                visible = visible & (lane + (part * LANES - (span - BLOCK)) <= sublane)
            masks.append(visible)
        mask = jnp.concatenate(masks, axis=1)
        scores, values = [], []
        for head in range(PER):
            columns = slice(LANES * head, LANES * head + 2 * LANES)
            query = queries_in[pl.ds(row, BLOCK), columns]
            inside = column < DQK if head == 0 else column >= 2 * LANES - DQK
            query = jnp.where(inside, query, jnp.zeros_like(query))
            scores.append(
                lax.dot_general(
                    query,
                    window[pl.ds(begin, span), columns],
                    (((1,), (1,)), ((), ())),
                    preferred_element_type=jnp.float32,
                )
            )
            values.append(window[pl.ds(begin, span), WQK + DV * head : WQK + DV * (head + 1)])
        scores = [jnp.where(mask, score, NEGATIVE) for score in scores]
        tops = [jnp.max(score, axis=1, keepdims=True) for score in scores]
        exponents = [jnp.exp((score - top) * scale) for score, top in zip(scores, tops)]
        totals = [jnp.sum(exponent, axis=1, keepdims=True) for exponent in exponents]
        weights = [
            (exponent * (1.0 / total)).astype(jnp.bfloat16)
            for exponent, total in zip(exponents, totals)
        ]
        for head in range(PER):
            mixed = jnp.dot(weights[head], values[head], preferred_element_type=jnp.float32)
            mixed_out[pl.ds(row, BLOCK), DV * head : DV * (head + 1)] = mixed.astype(jnp.bfloat16)

    def block(number, carry):
        row = pl.multiple_of(number * BLOCK, BLOCK)
        position = first_position + row
        start = latest_start(doc_starts, position + sublane)
        back = position - latest_start(doc_starts, position)
        shorter = 0
        for extra in EXTRA:
            pl.when((back > shorter) & (back <= extra) | (back == 0) & (shorter == 0))(
                functools.partial(heads, row, start, BLOCK + extra)
            )
            shorter = extra
        return carry

    lax.fori_loop(first, last, block, 0)


def attention_kernel(plan, doc_starts, place, *refs):
    query_table, key_table, order, query_count, key_count, part = plan
    queries, keys = refs[:query_count], refs[query_count : query_count + key_count]
    edge = refs[query_count + key_count]
    queries_in, window, mixed_out, sems, edge_sems = refs[-5:]
    targets = refs[-5 - (1 if order is None else SIDE) : -5]
    rows = queries_in.shape[0]
    block_rows = rows // GROUP
    copies = []
    for (ahead, aside), (array, at) in query_table.items():
        member = member_of(place, "yx", ahead, aside, -1)
        row = pl.multiple_of(member * block_rows, block_rows)
        top = member < SIDE
        query_wanted = {"all": True, "rest": ~top, "edge": top}[part]
        key_wanted = {"all": True, "rest": True, "edge": top}[part]
        copies.append(
            (
                query_wanted,
                pltpu.make_async_copy(
                    queries[array].at[at],
                    queries_in.at[pl.ds(row, block_rows)],
                    sems.at[0, ahead, aside],
                ),
            )
        )
        array, at = key_table[(ahead, aside)]
        copies.append(
            (
                key_wanted,
                pltpu.make_async_copy(
                    keys[array].at[at],
                    window.at[pl.ds(LONGEST + row, block_rows)],
                    sems.at[1, ahead, aside],
                ),
            )
        )
    if part != "rest":
        for aside in range(SIDE):
            row = pl.multiple_of(lax.rem(place[1] + SIDE - aside, SIDE) * block_rows, block_rows)
            copies.append(
                (
                    True,
                    pltpu.make_async_copy(
                        edge.at[aside], window.at[pl.ds(row, block_rows)], edge_sems.at[aside]
                    ),
                )
            )
    run_some(copies)
    border = LONGEST // BLOCK
    first = border if part == "rest" else 0
    last = border if part == "edge" else rows // BLOCK
    attend(doc_starts, place[2], queries_in, window, mixed_out, first, last)
    if order is None:
        run_copies([pltpu.make_async_copy(mixed_out, targets[0], edge_sems.at[0])])
        return
    copies = []
    for first in range(SIDE):
        for second in range(SIDE):
            member = member_of(place, order, first, second, 1)
            row = pl.multiple_of(member * block_rows, block_rows)
            top = member < SIDE
            copies.append(
                (
                    {"all": True, "rest": ~top, "edge": top}[part],
                    pltpu.make_async_copy(
                        mixed_out.at[pl.ds(row, block_rows)],
                        targets[first].at[second],
                        sems.at[0, first, second],
                    ),
                )
            )
    run_some(copies)


def attention(doc_starts, place, query, key_value, edge, order, part="all", whole=()):
    (queries, query_table), (keys, key_table) = query, key_value
    block_rows = keys[0].shape[1]
    rows = GROUP * block_rows
    plan = (query_table, key_table, order, len(queries), len(keys), part)
    outs = [(rows, WV)] if order is None else [(SIDE, block_rows, WV)] * SIDE
    operands = [doc_starts, place, *queries, *keys, edge]
    return pl.pallas_call(
        functools.partial(attention_kernel, plan),
        out_shape=[jax.ShapeDtypeStruct(shape, jnp.bfloat16) for shape in outs],
        in_specs=[SMEM, SMEM] + [ANY] * (len(operands) + len(whole) - 2),
        out_specs=[ANY] * len(outs),
        scratch_shapes=[
            pltpu.VMEM((rows, WQK), jnp.bfloat16),
            pltpu.VMEM((LONGEST + rows, WKV), jnp.bfloat16),
            pltpu.VMEM((rows, WV), jnp.bfloat16),
            pltpu.SemaphoreType.DMA((2, SIDE, SIDE)),
            pltpu.SemaphoreType.DMA((SIDE,)),
        ],
        input_output_aliases={len(operands) + i: i for i in range(len(whole))},
        name="attention",
    )(*operands, *whole)


def exchange(block):
    groups = [[half * GROUP + i for i in range(GROUP)] for half in range(2)]
    return lax.all_to_all(
        block, "seq", split_axis=0, concat_axis=0, axis_index_groups=groups, tiled=True
    )


def together(*arrays):
    return lax.optimization_barrier(arrays)


def local(queries, keys, values, doc_lengths):
    segment = lax.axis_index("pipe")
    segments = lax.axis_size("pipe")
    seq = lax.axis_index("seq")
    doc_starts = jnp.cumsum(doc_lengths, axis=1) - doc_lengths
    starts_here = lax.dynamic_index_in_dim(doc_starts, segment, 0, keepdims=False)
    starts_before = lax.dynamic_index_in_dim(
        doc_starts, (segment + segments - 1) % segments, 0, keepdims=False
    )
    rows = queries.shape[1]
    half, member = seq // GROUP, seq % GROUP
    place = jnp.stack([member // SIDE, member % SIDE, half * (GROUP * rows)]).astype(jnp.int32)
    columns = HEADS * DV
    second_qk, second_v = HEADS * DQK // 2, HEADS * DV // 2

    kv_first = pack(place, "xy", [(keys, 0, WQK), (values, 0, WV)])
    kv_first = first_stage(kv_first, "xy")
    kv_second = pack(place, "yx", [(keys, second_qk, WQK), (values, second_v, WV)])
    kv_second = first_stage(kv_second, "yx", True)
    q_second = shift(queries[:, :, second_qk:])
    queries, kv_first[1] = together(queries, kv_first[1])
    q_first = list(pack(place, "xy", [(queries, 0, WQK)]))
    kv_first[3], q_first[1] = together(kv_first[3], q_first[1])
    q_first = first_stage(q_first, "xy")
    q_second = first_stage(pack(place, "yx", [(q_second, 0, WQK)]), "yx")

    kv_first = second_stage(kv_first, "xy")
    kv_second = second_stage(kv_second, "yx")
    edge_first = send_edge(place, *kv_first)
    q_first = second_stage(q_first, "xy")
    edge_second = send_edge(place, *kv_second)
    q_second = second_stage(q_second, "yx")

    (out,) = attention(starts_here, place, q_first, kv_first, edge_first, None)
    out_first = exchange(out.reshape(GROUP, rows, WV))
    second = (starts_before, place, q_second, kv_second)
    out = attention(*second, kv_second[0][0], "yx", "rest")
    out = attention(*second, edge_second, "yx", "edge", tuple(out))
    out, table = second_stage(first_stage(out, "yx"), "yx")
    out_first = shift(out_first)
    whole = put(place, [out_first], None, 0, columns)
    return put(place, out, table, second_v, columns, whole)


def solution(mesh):
    placed = (P("pipe", "seq", None), P("pipe", "seq", None), P("pipe", "seq", None), P())
    return jax.shard_map(
        local, mesh=mesh, in_specs=placed, out_specs=P("pipe", "seq", None), check_vma=False
    )
```

```python
import functools
import jax
import jax.numpy as jnp
from jax import lax
from jax.experimental import pallas as pl
from jax.experimental.pallas import tpu as pltpu
from jax.sharding import PartitionSpec as P

HEADS = 64
DQK = 192
DV = 128
DOCS = 16
LONGEST = 512
BLOCK = 256
LANES = 128
EXTRA = (128, 256, 512)
CHUNKS = 2
SIDE = 4
GROUP = SIDE * SIDE
PER = HEADS // CHUNKS // GROUP
WQK = PER * DQK
WV = PER * DV
WKV = WQK + WV
NEGATIVE = -1e30
VMEM_LIMIT = 65500 * 1024
ANY = pl.BlockSpec(memory_space=pl.ANY)
SMEM = pl.BlockSpec(memory_space=pltpu.SMEM)


def run_copies(copies):
    for copy in copies:
        copy.start()
    for copy in copies:
        copy.wait()


def run_some(copies):
    for wanted, copy in copies:
        pl.when(wanted)(copy.start)
    for wanted, copy in copies:
        pl.when(wanted)(copy.wait)


def member_of(place, order, first, second, sign):
    ahead, aside = (second, first) if order == "xy" else (first, second)
    y = lax.rem(place[0] + SIDE + sign * ahead, SIDE)
    x = lax.rem(place[1] + SIDE + sign * aside, SIDE)
    return y * SIDE + x


def pack_kernel(plan, order, place, *refs):
    count = len(plan)
    sources, targets = refs[:count], refs[count : count + SIDE]
    buffer, in_sems, out_sems = refs[count + SIDE :]
    arriving, leaving = [], []
    for first in range(SIDE):
        group = []
        for second in range(SIDE):
            member = member_of(place, order, first, second, 1)
            for number, (source, (begin, width, at)) in enumerate(zip(sources, plan)):
                column = pl.multiple_of(begin + member * width, 128)
                group.append(
                    pltpu.make_async_copy(
                        source.at[0, :, pl.ds(column, width)],
                        buffer.at[first, second, :, pl.ds(at, width)],
                        in_sems.at[first, second, number],
                    )
                )
        arriving.append(group)
        leaving.append(pltpu.make_async_copy(buffer.at[first], targets[first], out_sems.at[first]))
    for group in arriving:
        for copy in group:
            copy.start()
    for first in range(SIDE):
        for copy in arriving[first]:
            copy.wait()
        leaving[first].start()
    for copy in leaving:
        copy.wait()


def pack(place, order, parts):
    rows = parts[0][0].shape[1]
    plan, at = [], 0
    for _, first, width in parts:
        plan.append((first, width, at))
        at += width
    return pl.pallas_call(
        functools.partial(pack_kernel, tuple(plan), order),
        out_shape=[jax.ShapeDtypeStruct((SIDE, rows, at), jnp.bfloat16)] * SIDE,
        in_specs=[SMEM] + [ANY] * len(parts),
        out_specs=[ANY] * SIDE,
        scratch_shapes=[
            pltpu.VMEM((SIDE, SIDE, rows, at), jnp.bfloat16),
            pltpu.SemaphoreType.DMA((SIDE, SIDE, len(parts))),
            pltpu.SemaphoreType.DMA((SIDE,)),
        ],
        compiler_params=pltpu.CompilerParams(vmem_limit_bytes=VMEM_LIMIT),
        name="pack",
    )(place, *[part[0] for part in parts])


def repack_kernel(begin, *refs):
    sources, targets = refs[:SIDE], refs[SIDE:-3]
    buffer, in_sems, out_sems = refs[-3:]
    count = SIDE - begin
    run_copies(
        [
            pltpu.make_async_copy(
                sources[first].at[pl.ds(begin, count)], buffer.at[:, first], in_sems.at[first]
            )
            for first in range(SIDE)
        ]
    )
    run_copies(
        [
            pltpu.make_async_copy(buffer.at[second], targets[second], out_sems.at[second])
            for second in range(count)
        ]
    )


def repack(arrays, begin):
    shape = arrays[0].shape
    count = SIDE - begin
    return pl.pallas_call(
        functools.partial(repack_kernel, begin),
        out_shape=[jax.ShapeDtypeStruct(shape, jnp.bfloat16)] * count,
        in_specs=[ANY] * SIDE,
        out_specs=[ANY] * count,
        scratch_shapes=[
            pltpu.VMEM((count,) + shape, jnp.bfloat16),
            pltpu.SemaphoreType.DMA((SIDE,)),
            pltpu.SemaphoreType.DMA((count,)),
        ],
        compiler_params=pltpu.CompilerParams(vmem_limit_bytes=VMEM_LIMIT),
        name="repack",
    )(*arrays)


def send(block, axis, distance, shifted=False):
    return routed(block, axis, distance, shifted)


def routed(block, axis, distance, shifted):
    routes = []
    for half in range(2):
        for y in range(SIDE):
            for x in range(SIDE):
                to_y = (y + distance) % SIDE if axis == "y" else y
                to_x = (x + distance) % SIDE if axis == "x" else x
                routes.append((half * GROUP + y * SIDE + x, half * GROUP + to_y * SIDE + to_x))
    if not shifted:
        return lax.ppermute(block, "seq", routes)
    segments, members = lax.axis_size("pipe"), lax.axis_size("seq")
    routes = [
        (segment * members + a, (segment + 1) % segments * members + b)
        for segment in range(segments)
        for a, b in routes
    ]
    return lax.ppermute(block, ("pipe", "seq"), routes)


def shift(block):
    segments = lax.axis_size("pipe")
    return lax.ppermute(block, "pipe", [(i, (i + 1) % segments) for i in range(segments)])


def first_stage(arrays, order, shifted=False):
    if shifted:
        return [send(array, order[0], i, True) for i, array in enumerate(arrays)]
    return [arrays[0]] + [send(arrays[i], order[0], i) for i in range(1, SIDE)]


def second_stage(arrays, order):
    got = [send(array, order[1], i + 1) for i, array in enumerate(repack(arrays, 1))]
    got = list(arrays) + got
    table = {}
    for first in range(SIDE):
        for second in range(SIDE):
            key = (second, first) if order == "xy" else (first, second)
            if second == 0:
                table[key] = (first, 0)
            else:
                table[key] = (SIDE + second - 1, first)
    return got, table


def edge_kernel(table, place, *refs):
    sources, (target, buffer, sems) = refs[:-3], refs[-3:]
    last = lax.rem(place[0] + 1, SIDE)
    for ahead in range(SIDE):

        @pl.when(last == ahead)
        def _():
            copies = []
            for aside in range(SIDE):
                array, at = table[(ahead, aside)]
                copies.append(
                    pltpu.make_async_copy(sources[array].at[at], buffer.at[aside], sems.at[aside])
                )
            run_copies(copies)

    run_copies([pltpu.make_async_copy(buffer, target, sems.at[0])])


def send_edge(place, arrays, table):
    shape = arrays[0].shape
    edge = pl.pallas_call(
        functools.partial(edge_kernel, table),
        out_shape=jax.ShapeDtypeStruct(shape, jnp.bfloat16),
        in_specs=[SMEM] + [ANY] * len(arrays),
        out_specs=ANY,
        scratch_shapes=[pltpu.VMEM(shape, jnp.bfloat16), pltpu.SemaphoreType.DMA((SIDE,))],
        compiler_params=pltpu.CompilerParams(vmem_limit_bytes=VMEM_LIMIT),
        name="edge",
    )(place, *arrays)
    return lax.ppermute(edge, "seq", [(i, i + GROUP) for i in range(GROUP)])


def place_kernel(first, table, place, *refs):
    target, buffer, in_sems, out_sem = refs[-4:]
    width = refs[0].shape[2]
    pieces = refs
    copies = []
    if table is None:
        table = {(0, at): (0, at) for at in range(GROUP)}
    for (ahead, aside), (array, at) in table.items():
        member = aside
        if pieces[0].shape[0] != GROUP:
            member = member_of(place, "yx", ahead, aside, -1)
        column = pl.multiple_of(member * width, 128)
        copies.append(
            pltpu.make_async_copy(
                pieces[array].at[at], buffer.at[:, pl.ds(column, width)], in_sems.at[array, at]
            )
        )
    run_copies(copies)
    run_copies(
        [pltpu.make_async_copy(buffer, target.at[0, :, pl.ds(first, GROUP * width)], out_sem.at[0])]
    )


def put(place, arrays, table, first, columns, whole=None):
    _, rows, width = arrays[0].shape
    extra = [] if whole is None else [whole]
    return pl.pallas_call(
        functools.partial(place_kernel, first, table),
        out_shape=jax.ShapeDtypeStruct((1, rows, columns), jnp.bfloat16),
        in_specs=[SMEM] + [ANY] * (len(arrays) + len(extra)),
        out_specs=ANY,
        scratch_shapes=[
            pltpu.VMEM((rows, GROUP * width), jnp.bfloat16),
            pltpu.SemaphoreType.DMA((len(arrays), GROUP)),
            pltpu.SemaphoreType.DMA((1,)),
        ],
        input_output_aliases={len(arrays) + 1: 0} if extra else {},
        compiler_params=pltpu.CompilerParams(vmem_limit_bytes=VMEM_LIMIT),
        name="place",
    )(place, *arrays, *extra)


def latest_start(doc_starts, position):
    start = jnp.zeros_like(position)
    for doc in range(1, DOCS):
        start = jnp.where(position >= doc_starts[doc], doc_starts[doc], start)
    return start


def attend(doc_starts, first_position, queries_in, window, mixed_out, first, last, extras):
    lane = lax.broadcasted_iota(jnp.int32, (BLOCK, LANES), 1)
    sublane = lax.broadcasted_iota(jnp.int32, (BLOCK, LANES), 0)
    column = lax.broadcasted_iota(jnp.int32, (BLOCK, 2 * LANES), 1)
    scale = DQK ** (-0.5)

    def heads(row, start, span):
        above = LONGEST + BLOCK - span
        begin = pl.multiple_of(row + above, LANES)
        start = start - (first_position + row - LONGEST + above)
        masks = []
        for part in range(span // LANES):
            visible = lane + part * LANES >= start
            if part * LANES >= span - BLOCK:
                visible = visible & (lane + (part * LANES - (span - BLOCK)) <= sublane)
            masks.append(visible)
        mask = jnp.concatenate(masks, axis=1)
        scores, values = [], []
        for head in range(PER):
            columns = slice(LANES * head, LANES * head + 2 * LANES)
            query = queries_in[pl.ds(row, BLOCK), columns]
            inside = column < DQK if head == 0 else column >= 2 * LANES - DQK
            query = jnp.where(inside, query, jnp.zeros_like(query))
            scores.append(
                lax.dot_general(
                    query,
                    window[pl.ds(begin, span), columns],
                    (((1,), (1,)), ((), ())),
                    preferred_element_type=jnp.float32,
                )
            )
            values.append(window[pl.ds(begin, span), WQK + DV * head : WQK + DV * (head + 1)])
        scores = [jnp.where(mask, score, NEGATIVE) for score in scores]
        tops = [jnp.max(score, axis=1, keepdims=True) for score in scores]
        exponents = [jnp.exp((score - top) * scale) for score, top in zip(scores, tops)]
        totals = [jnp.sum(exponent, axis=1, keepdims=True) for exponent in exponents]
        weights = [
            (exponent * (1.0 / total)).astype(jnp.bfloat16)
            for exponent, total in zip(exponents, totals)
        ]
        for head in range(PER):
            mixed = jnp.dot(weights[head], values[head], preferred_element_type=jnp.float32)
            mixed_out[pl.ds(row, BLOCK), DV * head : DV * (head + 1)] = mixed.astype(jnp.bfloat16)

    def block(number, carry):
        row = pl.multiple_of(number * BLOCK, BLOCK)
        position = first_position + row
        start = latest_start(doc_starts, position + sublane)
        back = position - latest_start(doc_starts, position)
        shorter = 0
        for extra in extras:
            pl.when((back > shorter) & (back <= extra) | (back == 0) & (shorter == 0))(
                functools.partial(heads, row, start, BLOCK + extra)
            )
            shorter = extra
        return carry

    lax.fori_loop(first, last, block, 0)


def attention_kernel(plan, doc_starts, place, *refs):
    query_table, key_table, order, query_count, key_count, part = plan
    queries, keys = refs[:query_count], refs[query_count : query_count + key_count]
    edge = refs[query_count + key_count]
    queries_in, window, mixed_out, sems, edge_sems = refs[-5:]
    targets = refs[-5 - (1 if order is None else SIDE) : -5]
    rows = queries_in.shape[0]
    block_rows = rows // GROUP
    copies = []
    for (ahead, aside), (array, at) in query_table.items():
        member = member_of(place, "yx", ahead, aside, -1)
        row = pl.multiple_of(member * block_rows, block_rows)
        top = member < SIDE
        query_wanted = {"all": True, "rest": ~top, "edge": top}[part]
        key_wanted = {"all": True, "rest": True, "edge": top}[part]
        copies.append(
            (
                query_wanted,
                pltpu.make_async_copy(
                    queries[array].at[at],
                    queries_in.at[pl.ds(row, block_rows)],
                    sems.at[0, ahead, aside],
                ),
            )
        )
        array, at = key_table[(ahead, aside)]
        copies.append(
            (
                key_wanted,
                pltpu.make_async_copy(
                    keys[array].at[at],
                    window.at[pl.ds(LONGEST + row, block_rows)],
                    sems.at[1, ahead, aside],
                ),
            )
        )
    if part != "rest":
        for aside in range(SIDE):
            row = pl.multiple_of(lax.rem(place[1] + SIDE - aside, SIDE) * block_rows, block_rows)
            copies.append(
                (
                    True,
                    pltpu.make_async_copy(
                        edge.at[aside], window.at[pl.ds(row, block_rows)], edge_sems.at[aside]
                    ),
                )
            )
    run_some(copies)
    border = LONGEST // BLOCK
    first = border if part == "rest" else 0
    last = border if part == "edge" else rows // BLOCK
    extras = EXTRA[-1:] if part == "edge" else EXTRA
    attend(doc_starts, place[2], queries_in, window, mixed_out, first, last, extras)
    if order is None:
        begin = LONGEST if part == "rest" else 0
        end = LONGEST if part == "edge" else rows
        span = pl.ds(begin, end - begin)
        run_copies([pltpu.make_async_copy(mixed_out.at[span], targets[0].at[span], edge_sems.at[0])])
        return
    copies = []
    for first in range(SIDE):
        for second in range(SIDE):
            member = member_of(place, order, first, second, 1)
            row = pl.multiple_of(member * block_rows, block_rows)
            top = member < SIDE
            copies.append(
                (
                    {"all": True, "rest": ~top, "edge": top}[part],
                    pltpu.make_async_copy(
                        mixed_out.at[pl.ds(row, block_rows)],
                        targets[first].at[second],
                        sems.at[0, first, second],
                    ),
                )
            )
    run_some(copies)


def attention(doc_starts, place, query, key_value, edge, order, part="all", whole=()):
    (queries, query_table), (keys, key_table) = query, key_value
    block_rows = keys[0].shape[1]
    rows = GROUP * block_rows
    plan = (query_table, key_table, order, len(queries), len(keys), part)
    outs = [(rows, WV)] if order is None else [(SIDE, block_rows, WV)] * SIDE
    operands = [doc_starts, place, *queries, *keys, edge]
    return pl.pallas_call(
        functools.partial(attention_kernel, plan),
        out_shape=[jax.ShapeDtypeStruct(shape, jnp.bfloat16) for shape in outs],
        in_specs=[SMEM, SMEM] + [ANY] * (len(operands) + len(whole) - 2),
        out_specs=[ANY] * len(outs),
        scratch_shapes=[
            pltpu.VMEM((rows, WQK), jnp.bfloat16),
            pltpu.VMEM((LONGEST + rows, WKV), jnp.bfloat16),
            pltpu.VMEM((rows, WV), jnp.bfloat16),
            pltpu.SemaphoreType.DMA((2, SIDE, SIDE)),
            pltpu.SemaphoreType.DMA((SIDE,)),
        ],
        input_output_aliases={len(operands) + i: i for i in range(len(whole))},
        compiler_params=pltpu.CompilerParams(vmem_limit_bytes=VMEM_LIMIT),
        name="attention",
    )(*operands, *whole)


def exchange(block):
    groups = [[half * GROUP + i for i in range(GROUP)] for half in range(2)]
    return lax.all_to_all(
        block, "seq", split_axis=0, concat_axis=0, axis_index_groups=groups, tiled=True
    )


def together(*arrays):
    return lax.optimization_barrier(arrays)


def local(queries, keys, values, doc_lengths):
    segment = lax.axis_index("pipe")
    segments = lax.axis_size("pipe")
    seq = lax.axis_index("seq")
    doc_starts = jnp.cumsum(doc_lengths, axis=1) - doc_lengths
    starts_here = lax.dynamic_index_in_dim(doc_starts, segment, 0, keepdims=False)
    starts_before = lax.dynamic_index_in_dim(
        doc_starts, (segment + segments - 1) % segments, 0, keepdims=False
    )
    rows = queries.shape[1]
    half, member = seq // GROUP, seq % GROUP
    place = jnp.stack([member // SIDE, member % SIDE, half * (GROUP * rows)]).astype(jnp.int32)
    columns = HEADS * DV
    second_qk, second_v = HEADS * DQK // 2, HEADS * DV // 2

    kv_first = pack(place, "xy", [(keys, 0, WQK), (values, 0, WV)])
    kv_first = first_stage(kv_first, "xy")
    kv_second = pack(place, "yx", [(keys, second_qk, WQK), (values, second_v, WV)])
    kv_second = first_stage(kv_second, "yx", True)
    q_second = shift(queries[:, :, second_qk:])
    queries, kv_first[1] = together(queries, kv_first[1])
    q_first = list(pack(place, "xy", [(queries, 0, WQK)]))
    kv_first[3], q_first[1] = together(kv_first[3], q_first[1])
    q_first = first_stage(q_first, "xy")
    q_second = list(pack(place, "yx", [(q_second, 0, WQK)]))

    kv_first = second_stage(kv_first, "xy")
    kv_first[0][-1], q_second[1] = together(kv_first[0][-1], q_second[1])
    q_second = first_stage(q_second, "yx")
    kv_second = second_stage(kv_second, "yx")
    edge_first = send_edge(place, *kv_first)
    q_first = second_stage(q_first, "xy")
    edge_second = send_edge(place, *kv_second)
    q_second = second_stage(q_second, "yx")

    first = (starts_here, place, q_first, kv_first)
    out = attention(*first, kv_first[0][0], None, "rest")
    (out,) = attention(*first, edge_first, None, "edge", tuple(out))
    out_first = exchange(out.reshape(GROUP, rows, WV))
    second = (starts_before, place, q_second, kv_second)
    out = attention(*second, kv_second[0][0], "yx", "rest")
    out = attention(*second, edge_second, "yx", "edge", tuple(out))
    out, table = second_stage(first_stage(out, "yx"), "yx")
    out_first = shift(out_first)
    whole = put(place, [out_first], None, 0, columns)
    return put(place, out, table, second_v, columns, whole)


def solution(mesh):
    placed = (P("pipe", "seq", None), P("pipe", "seq", None), P("pipe", "seq", None), P())
    return jax.shard_map(
        local, mesh=mesh, in_specs=placed, out_specs=P("pipe", "seq", None), check_vma=False
    )
```
